32 devices in a mesh: layer: 16 (over z, x, core), dp: 2 (over y).
Axes of the slice: x: 2, y: 2, z: 4, core: 2. Of those that a mesh axis runs over, the one named last changes fastest.
Arguments:
- weights: float32 [32, 1024, 1024], P('layer', 'dp'), may hold values from -6 to 6
- momentum: float32 [32, 1024, 1024], P('layer', 'dp'), may hold values from -3 to 3
- boundary: float32 [16, 512, 1024], P('layer', 'dp'), may hold values from -6 to 6
- adjoint: float32 [16, 512, 1024], P('layer', 'dp'), may hold values from -6 to 6
- target: float32 [512, 1024], P('dp'), may hold values from -6 to 6
Outputs:
- new_weights: float32 [32, 1024, 1024], P('layer', 'dp')
- new_momentum: float32 [32, 1024, 1024], P('layer', 'dp')
- new_boundary: float32 [16, 512, 1024], P('layer', 'dp')
- new_adjoint: float32 [16, 512, 1024], P('layer', 'dp')
The draws below stay inside these ranges and needn't reach their ends.
All inputs are finite; a program needn't handle non-finite values.
Results may differ from the reference program's by a relative error of at most 0.012.
Values may be sent and summed in bfloat16 or wider, within the bound.
A program may use at most 64 MiB of HBM per device.

```python
import math
import jax
import jax.numpy as jnp
from jax import lax

D = 1024
LPD = 2
STEPS = 2
SWEEPS = 2
GROUPS = 16
LAYERS = 32
ROWS = 512


def block_levels(key, shape, shards, smallest, high):
    loudness = 1.0
    for axis_at, blocks in shards:
        draws = jax.random.uniform(jax.random.fold_in(jax.random.fold_in(key, 6), axis_at), (blocks,), jnp.float32, smallest / len(shards), high / len(shards))
        loudness = loudness * jnp.repeat(jnp.exp(draws), shape[axis_at] // blocks).reshape((-1,) + (1,) * (len(shape) - 1 - axis_at))
    return loudness


def noise(key, extent, deviation, bound, split=(), kind=jnp.bfloat16):
    loudness = block_levels(key, extent, split, -0.22, 0.18) if split else 1.0
    values = jax.random.normal(key, extent, jnp.float32) * deviation * loudness
    return jnp.minimum(jnp.maximum(values, -bound), bound).astype(kind)


def setup_inputs(seed: int = 0) -> dict:
    seeds = jax.random.split(jax.random.key(seed), 6)
    weights = noise(seeds[0], (LAYERS, D, D), 1.0, 6.0, ((0, 16), (1, 2)), jnp.float32)
    momentum = noise(seeds[1], (LAYERS, D, D), 0.5, 3.0, ((0, 16), (1, 2)), jnp.float32)
    boundary = noise(seeds[2], (GROUPS, ROWS, D), 1.0, 6.0, ((0, 16), (1, 2)), jnp.float32)
    adjoint = noise(seeds[3], (GROUPS, ROWS, D), 1.0, 6.0, ((0, 16), (1, 2)), jnp.float32)
    target = noise(seeds[4], (ROWS, D), 1.0, 6.0, ((0, 2),), jnp.float32)
    return dict(weights=weights, momentum=momentum, boundary=boundary, adjoint=adjoint, target=target)


step_size = 0.5
momentum_decay = 0.9
learn_rate = 0.05

def forward_all(current, rounded_weights, width_scale):
    inputs_list = []
    slopes_list = []
    for layer_at in range(LPD):
        rounded = current.astype(jnp.bfloat16)
        product = jnp.einsum('grd,gde->gre', rounded.astype(jnp.float32), rounded_weights[:, layer_at].astype(jnp.float32), precision=lax.Precision.HIGHEST)
        squashed = jnp.tanh(product * width_scale)
        current = current + step_size * squashed
        inputs_list.append(rounded)
        slopes_list.append(squashed)
    return (current, inputs_list, slopes_list)

def backward_all(cotangent, rounded_weights, slopes_list, width_scale):
    for layer_at in reversed(range(LPD)):
        slope = slopes_list[layer_at]
        signal = (cotangent * (1.0 - slope * slope)).astype(jnp.bfloat16)
        pulled = jnp.einsum('gre,gde->grd', signal.astype(jnp.float32), rounded_weights[:, layer_at].astype(jnp.float32), precision=lax.Precision.HIGHEST)
        cotangent = cotangent + step_size * width_scale * pulled
    return cotangent

def gradient_all(cotangent, rounded_weights, inputs_list, slopes_list, width_scale, row_scale):
    grads = [None] * LPD
    for layer_at in reversed(range(LPD)):
        slope = slopes_list[layer_at]
        signal = (cotangent * (1.0 - slope * slope)).astype(jnp.bfloat16)
        grads[layer_at] = jnp.einsum('grd,gre->gde', inputs_list[layer_at].astype(jnp.float32), signal.astype(jnp.float32), precision=lax.Precision.HIGHEST) * row_scale
        if layer_at > 0:
            pulled = jnp.einsum('gre,gde->grd', signal.astype(jnp.float32), rounded_weights[:, layer_at].astype(jnp.float32), precision=lax.Precision.HIGHEST)
            cotangent = cotangent + step_size * width_scale * pulled
    return jnp.stack(grads, axis=1).reshape(LAYERS, D, D)

def reference(weights, momentum, boundary, adjoint, target):
    width_scale = 1.0 / math.sqrt(D)
    row_scale = 1.0 / math.sqrt(ROWS)
    current = boundary
    cotangent = adjoint
    for update_at in range(STEPS):
        rounded_weights = weights.astype(jnp.bfloat16).reshape(GROUPS, LPD, D, D)
        for sweep_at in range(SWEEPS):
            finals, inputs_list, slopes_list = forward_all(current, rounded_weights, width_scale)
            current = jnp.concatenate([current[:1], finals[:-1]], axis=0)
        finals, inputs_list, slopes_list = forward_all(current, rounded_weights, width_scale)
        missing = finals[-1] - target
        for sweep_at in range(SWEEPS):
            starts = backward_all(cotangent, rounded_weights, slopes_list, width_scale)
            cotangent = jnp.concatenate([starts[1:], missing[None]], axis=0)
        grads = gradient_all(cotangent, rounded_weights, inputs_list, slopes_list, width_scale, row_scale)
        momentum = momentum_decay * momentum + grads
        weights = weights - learn_rate * momentum
    return (weights, momentum, current, cotangent)
```

```python
import functools
import math

import jax
import jax.numpy as jnp
from jax import lax
from jax.experimental import pallas as pl
from jax.experimental.pallas import tpu as pltpu
from jax.sharding import PartitionSpec as P

STEPS = 2
SWEEPS = 2

step_size = 0.5
momentum_decay = 0.9
learn_rate = 0.05

MESH = pl.DeviceIdType.MESH
f32 = jnp.float32
bf16 = jnp.bfloat16


def kernel(
    groups, shards,
    w_in, m_in, b_in, a_in, t_in,
    wst, mst, xcur, acur, xs, mids, sigs,
    wfull, vfull, pulls, tgt, xw, in0, slopes, xb, ab, stage,
    load_sem, w_send, w_recv, v_send, v_recv, c_send, c_recv,
    hop_send, hop_recv, ex_send, ex_recv,
):
    layers, own, width = wst.shape
    rows = xcur.shape[0]
    tile = min(256, width)
    tiles = width // tile
    early = layers // 2
    g = lax.axis_index("layer")
    me = lax.axis_index("dp")
    is_first = g == 0
    is_last = g == groups - 1
    not_first = g > 0
    not_last = g < groups - 1
    width_scale = 1.0 / math.sqrt(width)
    row_scale = 1.0 / math.sqrt(rows * shards)

    def peer(d):
        return lax.rem(me + d, shards)

    def source(d):
        return lax.rem(me + shards - d, shards)

    loads = []
    for l in range(layers):
        loads.append(pltpu.make_async_copy(w_in.at[l], wst.at[l], load_sem.at[l]))
    loads.append(pltpu.make_async_copy(b_in.at[0], xcur, load_sem.at[layers]))
    loads.append(pltpu.make_async_copy(m_in, mst, load_sem.at[layers + 1]))
    loads.append(pltpu.make_async_copy(a_in.at[0], acur, load_sem.at[layers + 2]))
    loads.append(pltpu.make_async_copy(t_in, tgt, load_sem.at[layers + 3]))
    for c in loads:
        c.start()

    barrier = pltpu.get_barrier_semaphore()

    @pl.when(not_first)
    def _():
        pl.semaphore_signal(barrier, inc=1, device_id={"layer": g - 1}, device_id_type=MESH)

    @pl.when(not_last)
    def _():
        pl.semaphore_signal(barrier, inc=1, device_id={"layer": g + 1}, device_id_type=MESH)

    for d in range(1, shards):
        pl.semaphore_signal(barrier, inc=1, device_id={"dp": peer(d)}, device_id_type=MESH)

    own_rows = pl.ds(pl.multiple_of(me * own, own), own)

    def block_copy(buf, l, d, sends, recvs, sender):
        region = buf.at[l, pl.ds(pl.multiple_of(sender * own, own), own)]
        return pltpu.make_async_remote_copy(
            src_ref=region, dst_ref=region,
            send_sem=sends.at[l, d - 1], recv_sem=recvs.at[l, d - 1],
            device_id={"dp": peer(d)}, device_id_type=MESH,
        )

    neighbours = not_first.astype(jnp.int32) + not_last.astype(jnp.int32) + (shards - 1)
    for l in range(layers):
        loads[l].wait()
        wfull[l, own_rows, :] = wst[l].astype(bf16)
        if l == 0:
            pl.semaphore_wait(barrier, neighbours)
        for d in range(1, shards):
            block_copy(wfull, l, d, w_send, w_recv, me).start()
    def columns(j, n=tile):
        return pl.ds(pl.multiple_of(j * n, n), n)

    def tile_copy(l, d, j, sender):
        region = vfull.at[l, pl.ds(pl.multiple_of(sender * own, own), own), columns(j)]
        return pltpu.make_async_remote_copy(
            src_ref=region, dst_ref=region,
            send_sem=c_send.at[l - early, d - 1, j], recv_sem=c_recv.at[l - early, d - 1, j],
            device_id={"dp": peer(d)}, device_id_type=MESH,
        )

    loads[layers + 1].wait()
    for l in range(layers):
        vfull[l, own_rows, :] = (wst[l] - learn_rate * momentum_decay * mst[l]).astype(bf16)
    for l in range(early):
        for d in range(1, shards):
            block_copy(vfull, l, d, v_send, v_recv, me).start()
    for c in loads[layers:layers + 1] + loads[layers + 2:]:
        c.wait()

    def hop(t, way, s, j):
        slot = jnp.where(s == SWEEPS - 1, me, shards)
        into = (xb, ab)[way]
        return pltpu.make_async_remote_copy(
            src_ref=stage.at[way, s, :, columns(j)],
            dst_ref=into.at[t, slot, :, columns(j)],
            send_sem=hop_send.at[t, way, s, j], recv_sem=hop_recv.at[t, way, s, j],
            device_id={"layer": g + 1 if way == 0 else g - 1}, device_id_type=MESH,
        )

    def exchange(t, way, d, sender, j):
        into = (xb, ab)[way]
        region = into.at[t, sender, :, columns(j)]
        return pltpu.make_async_remote_copy(
            src_ref=region, dst_ref=region,
            send_sem=ex_send.at[t, way, d - 1, j], recv_sem=ex_recv.at[t, way, d - 1, j],
            device_id={"dp": peer(d)}, device_id_type=MESH,
        )

    def receive(t, way, s, expects):
        @pl.loop(0, tiles)
        def _(j):
            @pl.when(expects)
            def _():
                hop(t, way, s, j).wait_recv()

            @pl.when(s == SWEEPS - 1)
            def _():
                for d in range(1, shards):
                    exchange(t, way, d, me, j).start()

    def arrive(t, way, d, s):
        @pl.loop(0, tiles)
        def _(j):
            exchange(t, way, d, s, j).wait_recv()

    def fill(l, j):
        cols = columns(j)

        @pl.loop(1, shards)
        def _(d):
            tile_copy(l, d, j, source(d)).wait_recv()
            there = pl.ds(pl.multiple_of(source(d) * own, own), own)
            fresh = vfull[l, there, cols].astype(f32) - pulls[l - early, there, cols]
            wfull[l, there, cols] = fresh.astype(bf16)

    def forward(first_in, first_x, keep, emit, filling=None):
        for l in range(layers):
            last = l == layers - 1
            source_ref = first_in if l == 0 else keep.at[l - 1]
            fills = filling is not None and l >= early
            size = tile if fills or (last and emit is not None) else width

            @pl.loop(0, width // size, unroll=True)
            def _(j):
                if fills:
                    @pl.when(filling)
                    def _():
                        fill(l, j)

                cols = columns(j, size)
                product = jnp.dot(source_ref[...], wfull[l, :, cols], preferred_element_type=f32)
                squashed = jnp.tanh(product * width_scale)
                slopes[l, :, cols] = squashed
                before = first_x(cols) if l == 0 else xw[:, cols]
                after = before + step_size * squashed
                if last:
                    if emit is not None:
                        emit(j, cols, after)
                else:
                    xw[:, cols] = after
                    keep[l, :, cols] = after.astype(bf16)

    def backward(first_a, keep, emit):
        for l in reversed(range(layers)):
            start = first_a if l == layers - 1 else (lambda cols: xw[:, cols])

            every = pl.ds(0, width)
            slope = slopes[l]
            keep[l] = (start(every) * (1.0 - slope * slope)).astype(bf16)

            if l == 0 and emit is None:
                continue

            size = tile if l == 0 else width

            @pl.loop(0, width // size, unroll=True)
            def _(j):
                cols = columns(j, size)
                pulled = lax.dot_general(
                    keep[l], wfull[l, cols, :], (((1,), (1,)), ((), ())),
                    preferred_element_type=f32,
                )
                after = start(cols) + (step_size * width_scale) * pulled
                if l == 0:
                    emit(j, cols, after)
                else:
                    xw[:, cols] = after

    def own_x(cols):
        return xcur[:, cols]

    def own_a(cols):
        return acur[:, cols]

    for t in range(STEPS):
        own_mids = mids.at[me]
        own_sigs = sigs.at[me]
        if t == 0:
            for l in range(layers):
                for d in range(1, shards):
                    block_copy(wfull, l, d, w_send, w_recv, source(d)).wait_recv()

        @pl.when(is_first)
        def _():
            xb[t, me] = xcur[...].astype(bf16)

        @pl.loop(0, SWEEPS)
        def _(s):
            in0[...] = xcur[...].astype(bf16)

            def emit(j, cols, after):
                stage[0, s, :, cols] = after.astype(bf16)

                @pl.when(not_last)
                def _():
                    hop(t, 0, s, j).start()

            forward(in0, own_x, own_mids, emit, s == 0 if t > 0 else None)

            receive(t, 0, s, not_first)

            @pl.when(not_first)
            def _():
                slot = jnp.where(s == SWEEPS - 1, me, shards)
                xcur[...] = xb[t, slot].astype(f32)

        final_in = in0 if t < STEPS - 1 else xs.at[me]
        final_in[...] = xcur[...].astype(bf16)

        def finals(j, cols, after):
            @pl.when(is_last)
            def _():
                ab[t, me, :, cols] = (after - tgt[:, cols]).astype(bf16)

        forward(final_in, own_x, own_mids, finals)

        @pl.loop(0, SWEEPS)
        def _(s):
            def emit(j, cols, after):
                stage[1, s, :, cols] = after.astype(bf16)

                @pl.when(not_first)
                def _():
                    hop(t, 1, s, j).start()

            backward(own_a, own_sigs, emit)

            receive(t, 1, s, not_last)

            @pl.when(not_last)
            def _():
                slot = jnp.where(s == SWEEPS - 1, me, shards)
                acur[...] = ab[t, slot].astype(f32)

            @pl.when(is_last)
            def _():
                acur[...] = ab[t, me].astype(f32)

        if t == 0:
            for l in range(early, layers):
                for j in range(tiles):
                    for d in range(1, shards):
                        tile_copy(l, d, j, me).start()
        backward(own_a, own_sigs, None)

        @pl.loop(1, shards)
        def _(d):
            s = source(d)
            arrive(t, 0, d, s)
            if t == STEPS - 1:
                xs[s] = xb[t, s]
            forward(xb.at[t, s], lambda cols: xb[t, s, :, cols].astype(f32), mids.at[s], None)
            arrive(t, 1, d, s)
            backward(lambda cols: ab[t, s, :, cols].astype(f32), sigs.at[s], None)

        if t == 0:
            for l in range(layers):
                for d in range(1, shards):
                    block_copy(wfull, l, d, w_send, w_recv, me).wait_send()

        def gradient(l, at):
            feats = pl.ds(pl.multiple_of(at, own), own)
            if l == 0:
                left = xb[t, 0:shards, :, feats].reshape(shards * rows, own)
            else:
                left = mids[:, l - 1, :, feats].reshape(shards * rows, own)
            right = sigs[:, l].reshape(shards * rows, width)
            return lax.dot_general(
                left, right, (((0,), (0,)), ((), ())), preferred_element_type=f32
            ) * row_scale

        for l in range(layers if t < STEPS - 1 else 0):
            moved = momentum_decay * mst[l] + gradient(l, me * own)
            mst[l] = moved
            fresh = wst[l] - learn_rate * moved
            wst[l] = fresh
            wfull[l, own_rows, :] = fresh.astype(bf16)

        for l in range(layers if t < STEPS - 1 else 0):
            @pl.loop(1, shards)
            def _(d):
                there = pl.ds(pl.multiple_of(source(d) * own, own), own)
                pull = learn_rate * gradient(l, source(d) * own)
                if l < early:
                    block_copy(vfull, l, d, v_send, v_recv, source(d)).wait_recv()
                    wfull[l, there, :] = (vfull[l, there, :].astype(f32) - pull).astype(bf16)
                else:
                    pulls[l - early, there, :] = pull

        @pl.loop(0, SWEEPS)
        def _(s):
            @pl.loop(0, tiles)
            def _(j):
                @pl.when(not_last)
                def _():
                    hop(t, 0, s, j).wait_send()

                @pl.when(not_first)
                def _():
                    hop(t, 1, s, j).wait_send()

        for d in range(1, shards):
            @pl.loop(0, tiles)
            def _(j):
                exchange(t, 0, d, me, j).wait_send()
                exchange(t, 1, d, me, j).wait_send()

    for d in range(1, shards):
        for l in range(early):
            block_copy(vfull, l, d, v_send, v_recv, me).wait_send()
        for l in range(early, layers):
            for j in range(tiles):
                tile_copy(l, d, j, me).wait_send()


def finish(w, m, x, a, xs, mids, sigs, w_out, m_out, b_out, a_out, w_new, m_new, sem):
    layers, own, width = w.shape
    shards, rows, _ = xs.shape
    part = min(128, own)
    me = lax.axis_index("dp")
    row_scale = 1.0 / math.sqrt(rows * shards)
    copies = [
        pltpu.make_async_copy(x, b_out.at[0], sem.at[0]),
        pltpu.make_async_copy(a, a_out.at[0], sem.at[1]),
    ]
    for c in copies:
        c.start()
    for l in range(layers):
        for i in range(own // part):
            here = pl.ds(i * part, part)
            feats = pl.ds(pl.multiple_of(me * own + i * part, part), part)
            left = xs[:, :, feats] if l == 0 else mids[:, l - 1, :, feats]
            gradient = lax.dot_general(
                left.reshape(shards * rows, part), sigs[:, l].reshape(shards * rows, width),
                (((0,), (0,)), ((), ())), preferred_element_type=f32,
            ) * row_scale
            moved = momentum_decay * m[l, here, :] + gradient
            m_new[l, here, :] = moved
            w_new[l, here, :] = w[l, here, :] - learn_rate * moved
            at = 2 + 2 * (l * (own // part) + i)
            for k, (new, out) in enumerate(((m_new, m_out), (w_new, w_out))):
                c = pltpu.make_async_copy(new.at[l, here], out.at[l, here], sem.at[at + k])
                c.start()
                copies.append(c)
    for c in copies:
        c.wait()


def size_of(refs):
    return sum(math.prod(r.shape) * jnp.dtype(r.dtype).itemsize for r in refs)


def local(groups, shards, weights, momentum, boundary, adjoint, target):
    layers, own, width = weights.shape
    rows = target.shape[0]
    tiles = width // min(256, width)
    early = layers // 2
    others = max(shards - 1, 1)
    dma = pltpu.SemaphoreType.DMA
    anywhere = pl.BlockSpec(memory_space=pl.ANY)
    inside = pl.BlockSpec(memory_space=pltpu.VMEM)
    kept = (
        pltpu.VMEM((layers, own, width), f32),
        pltpu.VMEM((layers, own, width), f32),
        pltpu.VMEM((rows, width), f32),
        pltpu.VMEM((rows, width), f32),
        pltpu.VMEM((shards, rows, width), bf16),
        pltpu.VMEM((shards, max(layers - 1, 1), rows, width), bf16),
        pltpu.VMEM((shards, layers, rows, width), bf16),
    )
    scratch = [
        pltpu.VMEM((layers, width, width), bf16),
        pltpu.VMEM((layers, width, width), bf16),
        pltpu.VMEM((layers - early, width, width), f32),
        pltpu.VMEM((rows, width), f32),
        pltpu.VMEM((rows, width), f32),
        pltpu.VMEM((rows, width), bf16),
        pltpu.VMEM((layers, rows, width), f32),
        pltpu.VMEM((STEPS, shards + 1, rows, width), bf16),
        pltpu.VMEM((STEPS, shards + 1, rows, width), bf16),
        pltpu.VMEM((2, SWEEPS, rows, width), bf16),
    ]
    state = pl.pallas_call(
        functools.partial(kernel, groups, shards),
        out_shape=kept,
        in_specs=[pl.BlockSpec(memory_space=pltpu.HBM)] * 5,
        out_specs=(inside,) * len(kept),
        scratch_shapes=scratch + [
            dma((layers + 4,)),
            dma((layers, others)),
            dma((layers, others)),
            dma((layers, others)),
            dma((layers, others)),
            dma((layers - early, others, tiles)),
            dma((layers - early, others, tiles)),
            dma((STEPS, 2, SWEEPS, tiles)),
            dma((STEPS, 2, SWEEPS, tiles)),
            dma((STEPS, 2, others, tiles)),
            dma((STEPS, 2, others, tiles)),
        ],
        name="relax",
        compiler_params=pltpu.CompilerParams(
            collective_id=0, has_side_effects=True,
            vmem_limit_bytes=size_of(scratch) + 6 * 1024 * 1024,
        ),
    )(*(pltpu.with_memory_space_constraint(v, pltpu.HBM) for v in (weights, momentum, boundary, adjoint, target)))
    fresh = [pltpu.VMEM((layers, own, width), f32)] * 2
    return pl.pallas_call(
        finish,
        out_shape=tuple(
            jax.ShapeDtypeStruct(v.shape, f32) for v in (weights, momentum, boundary, adjoint)
        ),
        in_specs=[inside] * len(kept),
        out_specs=(anywhere,) * 4,
        scratch_shapes=fresh + [dma((2 + 2 * layers * max(own // 128, 1),))],
        name="finish",
        compiler_params=pltpu.CompilerParams(
            vmem_limit_bytes=size_of(fresh) + 8 * 1024 * 1024,
        ),
    )(*state)


def solution(mesh):
    placed = P("layer", "dp", None)
    return jax.shard_map(
        functools.partial(local, mesh.shape["layer"], mesh.shape["dp"]),
        mesh=mesh,
        in_specs=(placed,) * 4 + (P("dp", None),),
        out_specs=(placed,) * 4,
        check_vma=False,
    )
```

```python
import functools
import math

import jax
import jax.numpy as jnp
from jax import lax
from jax.experimental import pallas as pl
from jax.experimental.pallas import tpu as pltpu
from jax.sharding import PartitionSpec as P

STEPS = 2
SWEEPS = 2

step_size = 0.5
momentum_decay = 0.9
learn_rate = 0.05

MESH = pl.DeviceIdType.MESH
f32 = jnp.float32
bf16 = jnp.bfloat16


def kernel(
    groups, shards,
    w_in, m_in, b_in, a_in, t_in,
    wst, mst, xcur, acur, xs, mids, sigs,
    wfull, vfull, pulls, tgt, xw, in0, slopes, xb, ab, stage,
    load_sem, w_send, w_recv, v_send, v_recv, c_send, c_recv,
    hop_send, hop_recv, x_send, x_recv, a_send, a_recv,
):
    layers, own, width = wst.shape
    rows = xcur.shape[0]
    tile = min(512, width)
    tiles = width // tile
    strip = min(256, width)
    strips = width // strip
    halves = 2 if rows % 64 == 0 else 1
    half = rows // halves
    early = layers // 2
    g = lax.axis_index("layer")
    me = lax.axis_index("dp")
    is_first = g == 0
    is_last = g == groups - 1
    not_first = g > 0
    not_last = g < groups - 1
    width_scale = 1.0 / math.sqrt(width)
    row_scale = 1.0 / math.sqrt(rows * shards)

    def peer(d):
        return lax.rem(me + d, shards)

    def source(d):
        return lax.rem(me + shards - d, shards)

    loads = []
    for l in range(layers):
        loads.append(pltpu.make_async_copy(w_in.at[l], wst.at[l], load_sem.at[l]))
    loads.append(pltpu.make_async_copy(b_in.at[0], xcur, load_sem.at[layers]))
    loads.append(pltpu.make_async_copy(m_in, mst, load_sem.at[layers + 1]))
    loads.append(pltpu.make_async_copy(a_in.at[0], acur, load_sem.at[layers + 2]))
    loads.append(pltpu.make_async_copy(t_in, tgt, load_sem.at[layers + 3]))
    for c in loads:
        c.start()

    barrier = pltpu.get_barrier_semaphore()

    @pl.when(not_first)
    def _():
        pl.semaphore_signal(barrier, inc=1, device_id={"layer": g - 1}, device_id_type=MESH)

    @pl.when(not_last)
    def _():
        pl.semaphore_signal(barrier, inc=1, device_id={"layer": g + 1}, device_id_type=MESH)

    for d in range(1, shards):
        pl.semaphore_signal(barrier, inc=1, device_id={"dp": peer(d)}, device_id_type=MESH)

    own_rows = pl.ds(pl.multiple_of(me * own, own), own)

    def block_copy(buf, l, d, sends, recvs, sender):
        region = buf.at[l, pl.ds(pl.multiple_of(sender * own, own), own)]
        return pltpu.make_async_remote_copy(
            src_ref=region, dst_ref=region,
            send_sem=sends.at[l, d - 1], recv_sem=recvs.at[l, d - 1],
            device_id={"dp": peer(d)}, device_id_type=MESH,
        )

    neighbours = not_first.astype(jnp.int32) + not_last.astype(jnp.int32) + (shards - 1)
    for l in range(layers):
        loads[l].wait()
        wfull[l, own_rows, :] = wst[l].astype(bf16)
        if l == 0:
            pl.semaphore_wait(barrier, neighbours)
        for d in range(1, shards):
            block_copy(wfull, l, d, w_send, w_recv, me).start()
    def columns(j, n=tile):
        return pl.ds(pl.multiple_of(j * n, n), n)

    def tile_copy(l, d, j, sender):
        region = vfull.at[l, pl.ds(pl.multiple_of(sender * own, own), own), columns(j, strip)]
        return pltpu.make_async_remote_copy(
            src_ref=region, dst_ref=region,
            send_sem=c_send.at[l - early, d - 1, j], recv_sem=c_recv.at[l - early, d - 1, j],
            device_id={"dp": peer(d)}, device_id_type=MESH,
        )

    loads[layers + 1].wait()
    for l in range(layers):
        vfull[l, own_rows, :] = (wst[l] - learn_rate * momentum_decay * mst[l]).astype(bf16)
    for l in range(early):
        for d in range(1, shards):
            block_copy(vfull, l, d, v_send, v_recv, me).start()
    for c in loads[layers:layers + 1] + loads[layers + 2:]:
        c.wait()

    def part(h):
        return pl.ds(pl.multiple_of(h * half, half), half)

    def landing(s):
        return me if s == SWEEPS - 1 else shards

    def hop(t, way, s, h, j):
        into = (xb, ab)[way]
        return pltpu.make_async_remote_copy(
            src_ref=stage.at[way, s, part(h), columns(j)],
            dst_ref=into.at[t, landing(s), part(h), columns(j)],
            send_sem=hop_send.at[t, way, s, h, j], recv_sem=hop_recv.at[t, way, s, h, j],
            device_id={"layer": g + 1 if way == 0 else g - 1}, device_id_type=MESH,
        )

    def exchange_x(t, d, sender, h):
        region = xb.at[t, sender, part(h)]
        return pltpu.make_async_remote_copy(
            src_ref=region, dst_ref=region,
            send_sem=x_send.at[t, d - 1, h], recv_sem=x_recv.at[t, d - 1, h],
            device_id={"dp": peer(d)}, device_id_type=MESH,
        )

    def exchange_a(t, d, sender, h, j):
        region = ab.at[t, sender, part(h), columns(j)]
        return pltpu.make_async_remote_copy(
            src_ref=region, dst_ref=region,
            send_sem=a_send.at[t, d - 1, h, j], recv_sem=a_recv.at[t, d - 1, h, j],
            device_id={"dp": peer(d)}, device_id_type=MESH,
        )

    def take_x(t, s, h):
        @pl.when(not_first)
        def _():
            for j in range(tiles):
                hop(t, 0, s, h, j).wait_recv()

        if s == SWEEPS - 1:
            for d in range(1, shards):
                exchange_x(t, d, me, h).start()

        @pl.when(not_first)
        def _():
            xcur[part(h), :] = xb[t, landing(s), part(h)].astype(f32)

    def take_a(t, s, h):
        for j in range(tiles):
            @pl.when(not_last)
            def _():
                hop(t, 1, s, h, j).wait_recv()

            if s == SWEEPS - 1:
                for d in range(1, shards):
                    exchange_a(t, d, me, h, j).start()

        @pl.when(not_last)
        def _():
            acur[part(h), :] = ab[t, landing(s), part(h)].astype(f32)

        @pl.when(is_last)
        def _():
            acur[part(h), :] = ab[t, me, part(h)].astype(f32)

    def fill(l, j):
        cols = columns(j, strip)

        @pl.loop(1, shards)
        def _(d):
            tile_copy(l, d, j, source(d)).wait_recv()
            there = pl.ds(pl.multiple_of(source(d) * own, own), own)
            fresh = vfull[l, there, cols].astype(f32) - pulls[l - early, there, cols]
            wfull[l, there, cols] = fresh.astype(bf16)

    everything = pl.ds(0, rows)

    def forward(here, first_in, first_x, keep, emit, filling=False):
        for l in range(layers):
            last = l == layers - 1
            source_ref = first_in if l == 0 else keep.at[l - 1]
            fills = filling and l >= early
            size = strip if fills else tile if last and emit is not None else width

            for j in range(width // size):
                if fills:
                    fill(l, j)

                cols = columns(j, size)
                product = jnp.dot(source_ref[here, :], wfull[l, :, cols], preferred_element_type=f32)
                squashed = jnp.tanh(product * width_scale)
                slopes[l, here, cols] = squashed
                before = first_x(here, cols) if l == 0 else xw[here, cols]
                after = before + step_size * squashed
                if last:
                    if emit is not None:
                        emit(j, cols, after)
                else:
                    xw[here, cols] = after
                    keep[l, here, cols] = after.astype(bf16)

    def backward(here, first_a, keep, emit):
        for l in reversed(range(layers)):
            start = first_a if l == layers - 1 else (lambda here, cols: xw[here, cols])

            every = pl.ds(0, width)
            slope = slopes[l, here, :]
            keep[l, here, :] = (start(here, every) * (1.0 - slope * slope)).astype(bf16)

            if l == 0 and emit is None:
                continue

            size = tile if l == 0 else width

            for j in range(width // size):
                cols = columns(j, size)
                pulled = lax.dot_general(
                    keep[l, here, :], wfull[l, cols, :], (((1,), (1,)), ((), ())),
                    preferred_element_type=f32,
                )
                after = start(here, cols) + (step_size * width_scale) * pulled
                if l == 0:
                    emit(j, cols, after)
                else:
                    xw[here, cols] = after

    def own_x(here, cols):
        return xcur[here, cols]

    def own_a(here, cols):
        return acur[here, cols]

    for t in range(STEPS):
        own_mids = mids.at[me]
        own_sigs = sigs.at[me]
        if t == 0:
            for l in range(layers):
                for d in range(1, shards):
                    block_copy(wfull, l, d, w_send, w_recv, source(d)).wait_recv()

        @pl.when(is_first)
        def _():
            xb[t, me] = xcur[...].astype(bf16)

        def to_next(s, h, j):
            @pl.when(not_last)
            def _():
                hop(t, 0, s, h, j).start()

        if t > 0:
            in0[...] = xcur[...].astype(bf16)

            def emit(j, cols, after):
                stage[0, 0, :, cols] = after.astype(bf16)
                if (j + 1) * strip % tile == 0:
                    for h in range(halves):
                        to_next(0, h, j * strip // tile)

            forward(everything, in0, own_x, own_mids, emit, True)

        for s in range(0 if t == 0 else 1, SWEEPS):
            @pl.loop(0, halves)
            def _(h):
                if s > 0:
                    take_x(t, s - 1, h)
                in0[part(h), :] = xcur[part(h), :].astype(bf16)

                def emit(j, cols, after):
                    stage[0, s, part(h), cols] = after.astype(bf16)
                    to_next(s, h, j)

                forward(part(h), in0, own_x, own_mids, emit)

        final_in = in0 if t < STEPS - 1 else xs.at[me]

        def pull_back(s, h):
            def emit(j, cols, after):
                stage[1, s, part(h), cols] = after.astype(bf16)

                @pl.when(not_first)
                def _():
                    hop(t, 1, s, h, j).start()

            backward(part(h), own_a, own_sigs, emit)

        @pl.loop(0, halves)
        def _(h):
            take_x(t, SWEEPS - 1, h)
            final_in[part(h), :] = xcur[part(h), :].astype(bf16)

            def finals(j, cols, after):
                @pl.when(is_last)
                def _():
                    ab[t, me, part(h), cols] = (after - tgt[part(h), cols]).astype(bf16)

            forward(part(h), final_in, own_x, own_mids, finals)
            pull_back(0, h)

        for s in range(1, SWEEPS):
            @pl.loop(0, halves)
            def _(h):
                take_a(t, s - 1, h)
                pull_back(s, h)

        @pl.loop(0, halves)
        def _(h):
            take_a(t, SWEEPS - 1, h)

        if t == 0:
            for l in range(early, layers):
                for j in range(strips):
                    for d in range(1, shards):
                        tile_copy(l, d, j, me).start()
        backward(everything, own_a, own_sigs, None)

        @pl.loop(1, shards)
        def _(d):
            s = source(d)
            for h in range(halves):
                exchange_x(t, d, s, h).wait_recv()
            if t == STEPS - 1:
                xs[s] = xb[t, s]
            forward(
                everything, xb.at[t, s], lambda here, cols: xb[t, s, here, cols].astype(f32),
                mids.at[s], None,
            )

            @pl.loop(0, halves)
            def _(h):
                for j in range(tiles):
                    exchange_a(t, d, s, h, j).wait_recv()
                backward(
                    part(h), lambda here, cols: ab[t, s, here, cols].astype(f32), sigs.at[s], None
                )

        if t == 0:
            for l in range(layers):
                for d in range(1, shards):
                    block_copy(wfull, l, d, w_send, w_recv, me).wait_send()

        def gradient(l, at):
            feats = pl.ds(pl.multiple_of(at, own), own)
            if l == 0:
                left = xb[t, 0:shards, :, feats].reshape(shards * rows, own)
            else:
                left = mids[:, l - 1, :, feats].reshape(shards * rows, own)
            right = sigs[:, l].reshape(shards * rows, width)
            return lax.dot_general(
                left, right, (((0,), (0,)), ((), ())), preferred_element_type=f32
            ) * row_scale

        for l in range(layers if t < STEPS - 1 else 0):
            moved = momentum_decay * mst[l] + gradient(l, me * own)
            mst[l] = moved
            fresh = wst[l] - learn_rate * moved
            wst[l] = fresh
            wfull[l, own_rows, :] = fresh.astype(bf16)

        for l in range(layers if t < STEPS - 1 else 0):
            @pl.loop(1, shards)
            def _(d):
                there = pl.ds(pl.multiple_of(source(d) * own, own), own)
                pull = learn_rate * gradient(l, source(d) * own)
                if l < early:
                    block_copy(vfull, l, d, v_send, v_recv, source(d)).wait_recv()
                    wfull[l, there, :] = (vfull[l, there, :].astype(f32) - pull).astype(bf16)
                else:
                    pulls[l - early, there, :] = pull

        @pl.loop(0, halves)
        def _(h):
            for s in range(SWEEPS):
                for j in range(tiles):
                    @pl.when(not_last)
                    def _():
                        hop(t, 0, s, h, j).wait_send()

                    @pl.when(not_first)
                    def _():
                        hop(t, 1, s, h, j).wait_send()

            for d in range(1, shards):
                exchange_x(t, d, me, h).wait_send()
                for j in range(tiles):
                    exchange_a(t, d, me, h, j).wait_send()

    for d in range(1, shards):
        for l in range(early):
            block_copy(vfull, l, d, v_send, v_recv, me).wait_send()
        for l in range(early, layers):
            for j in range(strips):
                tile_copy(l, d, j, me).wait_send()


def finish(w, m, x, a, xs, mids, sigs, w_out, m_out, b_out, a_out, w_new, m_new, sem):
    layers, own, width = w.shape
    shards, rows, _ = xs.shape
    part = min(128, own)
    me = lax.axis_index("dp")
    row_scale = 1.0 / math.sqrt(rows * shards)
    copies = [
        pltpu.make_async_copy(x, b_out.at[0], sem.at[0]),
        pltpu.make_async_copy(a, a_out.at[0], sem.at[1]),
    ]
    for c in copies:
        c.start()
    for l in range(layers):
        for i in range(own // part):
            here = pl.ds(i * part, part)
            feats = pl.ds(pl.multiple_of(me * own + i * part, part), part)
            left = xs[:, :, feats] if l == 0 else mids[:, l - 1, :, feats]
            gradient = lax.dot_general(
                left.reshape(shards * rows, part), sigs[:, l].reshape(shards * rows, width),
                (((0,), (0,)), ((), ())), preferred_element_type=f32,
            ) * row_scale
            moved = momentum_decay * m[l, here, :] + gradient
            m_new[l, here, :] = moved
            w_new[l, here, :] = w[l, here, :] - learn_rate * moved
            at = 2 + 2 * (l * (own // part) + i)
            for k, (new, out) in enumerate(((m_new, m_out), (w_new, w_out))):
                c = pltpu.make_async_copy(new.at[l, here], out.at[l, here], sem.at[at + k])
                c.start()
                copies.append(c)
    for c in copies:
        c.wait()


def size_of(refs):
    return sum(math.prod(r.shape) * jnp.dtype(r.dtype).itemsize for r in refs)


def local(groups, shards, weights, momentum, boundary, adjoint, target):
    layers, own, width = weights.shape
    rows = target.shape[0]
    tiles = width // min(512, width)
    strips = width // min(256, width)
    halves = 2 if rows % 64 == 0 else 1
    early = layers // 2
    others = max(shards - 1, 1)
    dma = pltpu.SemaphoreType.DMA
    anywhere = pl.BlockSpec(memory_space=pl.ANY)
    inside = pl.BlockSpec(memory_space=pltpu.VMEM)
    kept = (
        pltpu.VMEM((layers, own, width), f32),
        pltpu.VMEM((layers, own, width), f32),
        pltpu.VMEM((rows, width), f32),
        pltpu.VMEM((rows, width), f32),
        pltpu.VMEM((shards, rows, width), bf16),
        pltpu.VMEM((shards, max(layers - 1, 1), rows, width), bf16),
        pltpu.VMEM((shards, layers, rows, width), bf16),
    )
    scratch = [
        pltpu.VMEM((layers, width, width), bf16),
        pltpu.VMEM((layers, width, width), bf16),
        pltpu.VMEM((layers - early, width, width), f32),
        pltpu.VMEM((rows, width), f32),
        pltpu.VMEM((rows, width), f32),
        pltpu.VMEM((rows, width), bf16),
        pltpu.VMEM((layers, rows, width), f32),
        pltpu.VMEM((STEPS, shards + 1, rows, width), bf16),
        pltpu.VMEM((STEPS, shards + 1, rows, width), bf16),
        pltpu.VMEM((2, SWEEPS, rows, width), bf16),
    ]
    state = pl.pallas_call(
        functools.partial(kernel, groups, shards),
        out_shape=kept,
        in_specs=[pl.BlockSpec(memory_space=pltpu.HBM)] * 5,
        out_specs=(inside,) * len(kept),
        scratch_shapes=scratch + [
            dma((layers + 4,)),
            dma((layers, others)),
            dma((layers, others)),
            dma((layers, others)),
            dma((layers, others)),
            dma((layers - early, others, strips)),
            dma((layers - early, others, strips)),
            dma((STEPS, 2, SWEEPS, halves, tiles)),
            dma((STEPS, 2, SWEEPS, halves, tiles)),
            dma((STEPS, others, halves)),
            dma((STEPS, others, halves)),
            dma((STEPS, others, halves, tiles)),
            dma((STEPS, others, halves, tiles)),
        ],
        name="relax",
        compiler_params=pltpu.CompilerParams(
            collective_id=0, has_side_effects=True,
            vmem_limit_bytes=size_of(scratch) + 6 * 1024 * 1024,
        ),
    )(*(pltpu.with_memory_space_constraint(v, pltpu.HBM) for v in (weights, momentum, boundary, adjoint, target)))
    fresh = [pltpu.VMEM((layers, own, width), f32)] * 2
    return pl.pallas_call(
        finish,
        out_shape=tuple(
            jax.ShapeDtypeStruct(v.shape, f32) for v in (weights, momentum, boundary, adjoint)
        ),
        in_specs=[inside] * len(kept),
        out_specs=(anywhere,) * 4,
        scratch_shapes=fresh + [dma((2 + 2 * layers * max(own // 128, 1),))],
        name="finish",
        compiler_params=pltpu.CompilerParams(
            vmem_limit_bytes=size_of(fresh) + 8 * 1024 * 1024,
        ),
    )(*state)


def solution(mesh):
    placed = P("layer", "dp", None)
    return jax.shard_map(
        functools.partial(local, mesh.shape["layer"], mesh.shape["dp"]),
        mesh=mesh,
        in_specs=(placed,) * 4 + (P("dp", None),),
        out_specs=(placed,) * 4,
        check_vma=False,
    )
```

```python
import functools
import math

import jax
import jax.numpy as jnp
from jax import lax
from jax.experimental import pallas as pl
from jax.experimental.pallas import tpu as pltpu
from jax.sharding import PartitionSpec as P

STEPS = 2
SWEEPS = 2

step_size = 0.5
momentum_decay = 0.9
learn_rate = 0.05

MESH = pl.DeviceIdType.MESH
f32 = jnp.float32
bf16 = jnp.bfloat16


def kernel(
    groups, shards,
    w_in, m_in, b_in, a_in, t_in,
    wst, mst, xcur, acur, xs, mids, sigs,
    wfull, wturn, vfull, pulls, tgt, xw, in0, slopes, xb, ab, stage,
    load_sem, w_send, w_recv, v_send, v_recv, c_send, c_recv,
    hop_send, hop_recv, strip_send, strip_recv, x_send, x_recv, a_send, a_recv,
):
    layers, own, width = wst.shape
    rows = xcur.shape[0]
    tile = min(512, width)
    tiles = width // tile
    strip = min(256, width)
    strips = width // strip
    halves = 2 if rows % 64 == 0 else 1
    half = rows // halves
    early = layers // 2
    g = lax.axis_index("layer")
    me = lax.axis_index("dp")
    is_first = g == 0
    is_last = g == groups - 1
    not_first = g > 0
    not_last = g < groups - 1
    width_scale = 1.0 / math.sqrt(width)
    row_scale = 1.0 / math.sqrt(rows * shards)

    def peer(d):
        return lax.rem(me + d, shards)

    def source(d):
        return lax.rem(me + shards - d, shards)

    loads = []
    for l in range(layers):
        loads.append(pltpu.make_async_copy(w_in.at[l], wst.at[l], load_sem.at[l]))
    loads.append(pltpu.make_async_copy(b_in.at[0], xcur, load_sem.at[layers]))
    loads.append(pltpu.make_async_copy(m_in, mst, load_sem.at[layers + 1]))
    loads.append(pltpu.make_async_copy(a_in.at[0], acur, load_sem.at[layers + 2]))
    loads.append(pltpu.make_async_copy(t_in, tgt, load_sem.at[layers + 3]))
    for c in loads:
        c.start()

    barrier = pltpu.get_barrier_semaphore()

    @pl.when(not_first)
    def _():
        pl.semaphore_signal(barrier, inc=1, device_id={"layer": g - 1}, device_id_type=MESH)

    @pl.when(not_last)
    def _():
        pl.semaphore_signal(barrier, inc=1, device_id={"layer": g + 1}, device_id_type=MESH)

    for d in range(1, shards):
        pl.semaphore_signal(barrier, inc=1, device_id={"dp": peer(d)}, device_id_type=MESH)

    own_rows = pl.ds(pl.multiple_of(me * own, own), own)

    def block_copy(buf, l, d, sends, recvs, sender):
        region = buf.at[l, pl.ds(pl.multiple_of(sender * own, own), own)]
        return pltpu.make_async_remote_copy(
            src_ref=region, dst_ref=region,
            send_sem=sends.at[l, d - 1], recv_sem=recvs.at[l, d - 1],
            device_id={"dp": peer(d)}, device_id_type=MESH,
        )

    neighbours = not_first.astype(jnp.int32) + not_last.astype(jnp.int32) + (shards - 1)
    for l in range(layers):
        loads[l].wait()
        wfull[l, own_rows, :] = wst[l].astype(bf16)
        if l == 0:
            pl.semaphore_wait(barrier, neighbours)
        for d in range(1, shards):
            block_copy(wfull, l, d, w_send, w_recv, me).start()
    def columns(j, n=tile):
        return pl.ds(pl.multiple_of(j * n, n), n)

    def tile_copy(l, d, j, sender):
        region = vfull.at[l, pl.ds(pl.multiple_of(sender * own, own), own), columns(j, strip)]
        return pltpu.make_async_remote_copy(
            src_ref=region, dst_ref=region,
            send_sem=c_send.at[l - early, d - 1, j], recv_sem=c_recv.at[l - early, d - 1, j],
            device_id={"dp": peer(d)}, device_id_type=MESH,
        )

    loads[layers + 1].wait()
    for l in range(layers):
        vfull[l, own_rows, :] = (wst[l] - learn_rate * momentum_decay * mst[l]).astype(bf16)
    for l in range(early):
        for d in range(1, shards):
            block_copy(vfull, l, d, v_send, v_recv, me).start()
    for c in loads[layers:layers + 1] + loads[layers + 2:]:
        c.wait()

    def part(h):
        return pl.ds(pl.multiple_of(h * half, half), half)

    def landing(s):
        return me if s == SWEEPS - 1 else shards

    def hop(t, way, s, h, j):
        into = (xb, ab)[way]
        return pltpu.make_async_remote_copy(
            src_ref=stage.at[way, s, part(h), columns(j)],
            dst_ref=into.at[t, landing(s), part(h), columns(j)],
            send_sem=hop_send.at[t, way, s, h, j], recv_sem=hop_recv.at[t, way, s, h, j],
            device_id={"layer": g + 1 if way == 0 else g - 1}, device_id_type=MESH,
        )

    def strip_hop(t, j):
        return pltpu.make_async_remote_copy(
            src_ref=stage.at[0, 0, :, columns(j, strip)],
            dst_ref=xb.at[t, landing(0), :, columns(j, strip)],
            send_sem=strip_send.at[t, j], recv_sem=strip_recv.at[t, j],
            device_id={"layer": g + 1}, device_id_type=MESH,
        )

    def exchange_x(t, d, sender, h):
        region = xb.at[t, sender, part(h)]
        return pltpu.make_async_remote_copy(
            src_ref=region, dst_ref=region,
            send_sem=x_send.at[t, d - 1, h], recv_sem=x_recv.at[t, d - 1, h],
            device_id={"dp": peer(d)}, device_id_type=MESH,
        )

    def exchange_a(t, d, sender, h, j):
        region = ab.at[t, sender, part(h), columns(j)]
        return pltpu.make_async_remote_copy(
            src_ref=region, dst_ref=region,
            send_sem=a_send.at[t, d - 1, h, j], recv_sem=a_recv.at[t, d - 1, h, j],
            device_id={"dp": peer(d)}, device_id_type=MESH,
        )

    def take_x(t, s, h):
        if t == 0 or s > 0:
            @pl.when(not_first)
            def _():
                for j in range(tiles):
                    hop(t, 0, s, h, j).wait_recv()

        if s == SWEEPS - 1:
            for d in range(1, shards):
                exchange_x(t, d, me, h).start()

        @pl.when(not_first)
        def _():
            xcur[part(h), :] = xb[t, landing(s), part(h)].astype(f32)

    def take_a(t, s, h):
        for j in range(tiles):
            @pl.when(not_last)
            def _():
                hop(t, 1, s, h, j).wait_recv()

            if s == SWEEPS - 1:
                for d in range(1, shards):
                    exchange_a(t, d, me, h, j).start()

        @pl.when(not_last)
        def _():
            acur[part(h), :] = ab[t, landing(s), part(h)].astype(f32)

        @pl.when(is_last)
        def _():
            acur[part(h), :] = ab[t, me, part(h)].astype(f32)

    def fill(l, j):
        cols = columns(j, strip)

        @pl.loop(1, shards)
        def _(d):
            tile_copy(l, d, j, source(d)).wait_recv()
            there = pl.ds(pl.multiple_of(source(d) * own, own), own)
            fresh = vfull[l, there, cols].astype(f32) - pulls[l - early, there, cols]
            wfull[l, there, cols] = fresh.astype(bf16)

    def turn(l, j):
        @pl.loop(1, shards)
        def _(d):
            there = pl.ds(pl.multiple_of(source(d) * own, own), own)
            wturn[l, columns(j, strip), there] = wfull[l, there, columns(j, strip)].T

    everything = pl.ds(0, rows)

    def forward(here, first_in, first_x, keep, emit, filling=False):
        for l in range(layers):
            last = l == layers - 1
            source_ref = first_in if l == 0 else keep.at[l - 1]
            fills = filling and l >= early
            size = strip if fills else tile if last and emit is not None else width

            for j in range(width // size):
                if fills:
                    fill(l, j)

                cols = columns(j, size)
                product = jnp.dot(source_ref[here, :], wfull[l, :, cols], preferred_element_type=f32)
                squashed = jnp.tanh(product * width_scale)
                slopes[l, here, cols] = squashed
                before = first_x(here, cols) if l == 0 else xw[here, cols]
                after = before + step_size * squashed
                if last:
                    if emit is not None:
                        emit(j, cols, after)
                else:
                    xw[here, cols] = after
                    keep[l, here, cols] = after.astype(bf16)

                if fills:
                    turn(l, j)

    def backward(t, here, first_a, keep, emit):
        for l in reversed(range(layers)):
            start = first_a if l == layers - 1 else (lambda here, cols: xw[here, cols])

            every = pl.ds(0, width)
            slope = slopes[l, here, :]
            keep[l, here, :] = (start(here, every) * (1.0 - slope * slope)).astype(bf16)

            if l == 0 and emit is None:
                continue

            size = tile if l == 0 else width

            for j in range(width // size):
                cols = columns(j, size)
                if t > 0:
                    pulled = jnp.dot(
                        keep[l, here, :], wturn[l, :, cols], preferred_element_type=f32
                    )
                else:
                    pulled = lax.dot_general(
                        keep[l, here, :], wfull[l, cols, :], (((1,), (1,)), ((), ())),
                        preferred_element_type=f32,
                    )
                after = start(here, cols) + (step_size * width_scale) * pulled
                if l == 0:
                    emit(j, cols, after)
                else:
                    xw[here, cols] = after

    def own_x(here, cols):
        return xcur[here, cols]

    def own_a(here, cols):
        return acur[here, cols]

    for t in range(STEPS):
        own_mids = mids.at[me]
        own_sigs = sigs.at[me]
        if t == 0:
            for l in range(layers):
                for d in range(1, shards):
                    block_copy(wfull, l, d, w_send, w_recv, source(d)).wait_recv()

        @pl.when(is_first)
        def _():
            xb[t, me] = xcur[...].astype(bf16)

        def to_next(s, h, j):
            @pl.when(not_last)
            def _():
                hop(t, 0, s, h, j).start()

        if t > 0:
            in0[...] = xcur[...].astype(bf16)

            def emit(j, cols, after):
                stage[0, 0, :, cols] = after.astype(bf16)

                @pl.when(not_last)
                def _():
                    strip_hop(t, j).start()

            forward(everything, in0, own_x, own_mids, emit, True)

            @pl.when(not_first)
            def _():
                for j in range(strips):
                    strip_hop(t, j).wait_recv()

        for s in range(0 if t == 0 else 1, SWEEPS):
            @pl.loop(0, halves)
            def _(h):
                if s > 0:
                    take_x(t, s - 1, h)
                in0[part(h), :] = xcur[part(h), :].astype(bf16)

                def emit(j, cols, after):
                    stage[0, s, part(h), cols] = after.astype(bf16)
                    to_next(s, h, j)

                forward(part(h), in0, own_x, own_mids, emit)

        def pull_back(s, h):
            def emit(j, cols, after):
                stage[1, s, part(h), cols] = after.astype(bf16)

                @pl.when(not_first)
                def _():
                    hop(t, 1, s, h, j).start()

            backward(t, part(h), own_a, own_sigs, emit)

        @pl.loop(0, halves)
        def _(h):
            take_x(t, SWEEPS - 1, h)
            in0[part(h), :] = xcur[part(h), :].astype(bf16)
            if t == STEPS - 1:
                xs[me, part(h)] = in0[part(h), own_rows]

            def finals(j, cols, after):
                @pl.when(is_last)
                def _():
                    ab[t, me, part(h), cols] = (after - tgt[part(h), cols]).astype(bf16)

            forward(part(h), in0, own_x, own_mids, finals)
            pull_back(0, h)

        for s in range(1, SWEEPS):
            @pl.loop(0, halves)
            def _(h):
                take_a(t, s - 1, h)
                pull_back(s, h)

        @pl.loop(0, halves)
        def _(h):
            take_a(t, SWEEPS - 1, h)

        if t == 0:
            for l in range(early, layers):
                for j in range(strips):
                    for d in range(1, shards):
                        tile_copy(l, d, j, me).start()
        backward(t, everything, own_a, own_sigs, None)

        @pl.loop(1, shards)
        def _(d):
            s = source(d)
            for h in range(halves):
                exchange_x(t, d, s, h).wait_recv()
            if t == STEPS - 1:
                xs[s] = xb[t, s, :, own_rows]
            forward(
                everything, xb.at[t, s], lambda here, cols: xb[t, s, here, cols].astype(f32),
                mids.at[s], None,
            )

            @pl.loop(0, halves)
            def _(h):
                for j in range(tiles):
                    exchange_a(t, d, s, h, j).wait_recv()
                backward(
                    t, part(h), lambda here, cols: ab[t, s, here, cols].astype(f32), sigs.at[s], None
                )

        if t == 0:
            for l in range(layers):
                for d in range(1, shards):
                    block_copy(wfull, l, d, w_send, w_recv, me).wait_send()

        def gradient(l, at):
            feats = pl.ds(pl.multiple_of(at, own), own)
            if l == 0:
                left = xb[t, 0:shards, :, feats].reshape(shards * rows, own)
            else:
                left = mids[:, l - 1, :, feats].reshape(shards * rows, own)
            right = sigs[:, l].reshape(shards * rows, width)
            return lax.dot_general(
                left, right, (((0,), (0,)), ((), ())), preferred_element_type=f32
            ) * row_scale

        for l in range(layers if t < STEPS - 1 else 0):
            moved = momentum_decay * mst[l] + gradient(l, me * own)
            mst[l] = moved
            fresh = wst[l] - learn_rate * moved
            wst[l] = fresh
            wfull[l, own_rows, :] = fresh.astype(bf16)
            wturn[l, :, own_rows] = wfull[l, own_rows, :].T

        for l in range(layers if t < STEPS - 1 else 0):
            @pl.loop(1, shards)
            def _(d):
                there = pl.ds(pl.multiple_of(source(d) * own, own), own)
                pull = learn_rate * gradient(l, source(d) * own)
                if l < early:
                    block_copy(vfull, l, d, v_send, v_recv, source(d)).wait_recv()
                    wfull[l, there, :] = (vfull[l, there, :].astype(f32) - pull).astype(bf16)
                    wturn[l, :, there] = wfull[l, there, :].T
                else:
                    pulls[l - early, there, :] = pull

        @pl.loop(0, halves)
        def _(h):
            for s in range(SWEEPS):
                for j in range(tiles):
                    if t == 0 or s > 0:
                        @pl.when(not_last)
                        def _():
                            hop(t, 0, s, h, j).wait_send()

                    @pl.when(not_first)
                    def _():
                        hop(t, 1, s, h, j).wait_send()

            for d in range(1, shards):
                exchange_x(t, d, me, h).wait_send()
                for j in range(tiles):
                    exchange_a(t, d, me, h, j).wait_send()

        if t > 0:
            @pl.when(not_last)
            def _():
                for j in range(strips):
                    strip_hop(t, j).wait_send()

    for d in range(1, shards):
        for l in range(early):
            block_copy(vfull, l, d, v_send, v_recv, me).wait_send()
        for l in range(early, layers):
            for j in range(strips):
                tile_copy(l, d, j, me).wait_send()


def finish(w, m, x, a, xs, mids, sigs, w_out, m_out, b_out, a_out, w_new, m_new, sem):
    layers, own, width = w.shape
    shards, rows, _ = mids.shape[0], *mids.shape[2:]
    part = min(128, own)
    me = lax.axis_index("dp")
    row_scale = 1.0 / math.sqrt(rows * shards)
    copies = [
        pltpu.make_async_copy(x, b_out.at[0], sem.at[0]),
        pltpu.make_async_copy(a, a_out.at[0], sem.at[1]),
    ]
    for c in copies:
        c.start()
    for l in range(layers):
        for i in range(own // part):
            here = pl.ds(i * part, part)
            feats = pl.ds(pl.multiple_of(me * own + i * part, part), part)
            left = xs[:, :, here] if l == 0 else mids[:, l - 1, :, feats]
            gradient = lax.dot_general(
                left.reshape(shards * rows, part), sigs[:, l].reshape(shards * rows, width),
                (((0,), (0,)), ((), ())), preferred_element_type=f32,
            ) * row_scale
            moved = momentum_decay * m[l, here, :] + gradient
            m_new[l, here, :] = moved
            w_new[l, here, :] = w[l, here, :] - learn_rate * moved
            at = 2 + 2 * (l * (own // part) + i)
            for k, (new, out) in enumerate(((m_new, m_out), (w_new, w_out))):
                c = pltpu.make_async_copy(new.at[l, here], out.at[l, here], sem.at[at + k])
                c.start()
                copies.append(c)
    for c in copies:
        c.wait()


def size_of(refs):
    return sum(math.prod(r.shape) * jnp.dtype(r.dtype).itemsize for r in refs)


def local(groups, shards, weights, momentum, boundary, adjoint, target):
    layers, own, width = weights.shape
    rows = target.shape[0]
    tiles = width // min(512, width)
    strips = width // min(256, width)
    halves = 2 if rows % 64 == 0 else 1
    early = layers // 2
    others = max(shards - 1, 1)
    dma = pltpu.SemaphoreType.DMA
    anywhere = pl.BlockSpec(memory_space=pl.ANY)
    inside = pl.BlockSpec(memory_space=pltpu.VMEM)
    kept = (
        pltpu.VMEM((layers, own, width), f32),
        pltpu.VMEM((layers, own, width), f32),
        pltpu.VMEM((rows, width), f32),
        pltpu.VMEM((rows, width), f32),
        pltpu.VMEM((shards, rows, own), bf16),
        pltpu.VMEM((shards, max(layers - 1, 1), rows, width), bf16),
        pltpu.VMEM((shards, layers, rows, width), bf16),
    )
    scratch = [
        pltpu.VMEM((layers, width, width), bf16),
        pltpu.VMEM((layers, width, width), bf16),
        pltpu.VMEM((layers, width, width), bf16),
        pltpu.VMEM((layers - early, width, width), f32),
        pltpu.VMEM((rows, width), f32),
        pltpu.VMEM((rows, width), f32),
        pltpu.VMEM((rows, width), bf16),
        pltpu.VMEM((layers, rows, width), f32),
        pltpu.VMEM((STEPS, shards + 1, rows, width), bf16),
        pltpu.VMEM((STEPS, shards + 1, rows, width), bf16),
        pltpu.VMEM((2, SWEEPS, rows, width), bf16),
    ]
    state = pl.pallas_call(
        functools.partial(kernel, groups, shards),
        out_shape=kept,
        in_specs=[pl.BlockSpec(memory_space=pltpu.HBM)] * 5,
        out_specs=(inside,) * len(kept),
        scratch_shapes=scratch + [
            dma((layers + 4,)),
            dma((layers, others)),
            dma((layers, others)),
            dma((layers, others)),
            dma((layers, others)),
            dma((layers - early, others, strips)),
            dma((layers - early, others, strips)),
            dma((STEPS, 2, SWEEPS, halves, tiles)),
            dma((STEPS, 2, SWEEPS, halves, tiles)),
            dma((STEPS, strips)),
            dma((STEPS, strips)),
            dma((STEPS, others, halves)),
            dma((STEPS, others, halves)),
            dma((STEPS, others, halves, tiles)),
            dma((STEPS, others, halves, tiles)),
        ],
        name="relax",
        compiler_params=pltpu.CompilerParams(
            collective_id=0, has_side_effects=True,
            vmem_limit_bytes=min(size_of(scratch) + 12 * 2**20, 63 * 2**20 - size_of(kept)),
        ),
    )(*(pltpu.with_memory_space_constraint(v, pltpu.HBM) for v in (weights, momentum, boundary, adjoint, target)))
    fresh = [pltpu.VMEM((layers, own, width), f32)] * 2
    return pl.pallas_call(
        finish,
        out_shape=tuple(
            jax.ShapeDtypeStruct(v.shape, f32) for v in (weights, momentum, boundary, adjoint)
        ),
        in_specs=[inside] * len(kept),
        out_specs=(anywhere,) * 4,
        scratch_shapes=fresh + [dma((2 + 2 * layers * max(own // 128, 1),))],
        name="finish",
        compiler_params=pltpu.CompilerParams(
            vmem_limit_bytes=size_of(fresh) + 8 * 1024 * 1024,
        ),
    )(*state)


def solution(mesh):
    placed = P("layer", "dp", None)
    return jax.shard_map(
        functools.partial(local, mesh.shape["layer"], mesh.shape["dp"]),
        mesh=mesh,
        in_specs=(placed,) * 4 + (P("dp", None),),
        out_specs=(placed,) * 4,
        check_vma=False,
    )
```

```python
import functools
import math

import jax
import jax.numpy as jnp
from jax import lax
from jax.experimental import pallas as pl
from jax.experimental.pallas import tpu as pltpu
from jax.sharding import PartitionSpec as P

STEPS = 2
SWEEPS = 2

step_size = 0.5
momentum_decay = 0.9
learn_rate = 0.05

MESH = pl.DeviceIdType.MESH
f32 = jnp.float32
bf16 = jnp.bfloat16


def kernel(
    groups, shards,
    w_in, m_in, b_in, a_in, t_in,
    wst, mst, xcur, acur, xs, mids, sigs,
    wfull, wturn, vfull, pulls, tgt, xw, in0, slopes, xb, ab, stage,
    load_sem, w_send, w_recv, v_send, v_recv, c_send, c_recv,
    hop_send, hop_recv, strip_send, strip_recv, x_send, x_recv, a_send, a_recv,
):
    layers, own, width = wst.shape
    rows = xcur.shape[0]
    tile = min(512, width)
    tiles = width // tile
    strip = min(256, width)
    strips = width // strip
    halves = 2 if rows % 64 == 0 else 1
    half = rows // halves
    early = layers // 2
    g = lax.axis_index("layer")
    me = lax.axis_index("dp")
    is_first = g == 0
    is_last = g == groups - 1
    not_first = g > 0
    not_last = g < groups - 1
    width_scale = 1.0 / math.sqrt(width)
    row_scale = 1.0 / math.sqrt(rows * shards)

    def peer(d):
        return lax.rem(me + d, shards)

    def source(d):
        return lax.rem(me + shards - d, shards)

    loads = []
    for l in range(layers):
        loads.append(pltpu.make_async_copy(w_in.at[l], wst.at[l], load_sem.at[l]))
    loads.append(pltpu.make_async_copy(b_in.at[0], xcur, load_sem.at[layers]))
    loads.append(pltpu.make_async_copy(m_in, mst, load_sem.at[layers + 1]))
    loads.append(pltpu.make_async_copy(a_in.at[0], acur, load_sem.at[layers + 2]))
    loads.append(pltpu.make_async_copy(t_in, tgt, load_sem.at[layers + 3]))
    for c in loads:
        c.start()

    barrier = pltpu.get_barrier_semaphore()

    @pl.when(not_first)
    def _():
        pl.semaphore_signal(barrier, inc=1, device_id={"layer": g - 1}, device_id_type=MESH)

    @pl.when(not_last)
    def _():
        pl.semaphore_signal(barrier, inc=1, device_id={"layer": g + 1}, device_id_type=MESH)

    for d in range(1, shards):
        pl.semaphore_signal(barrier, inc=1, device_id={"dp": peer(d)}, device_id_type=MESH)

    own_rows = pl.ds(pl.multiple_of(me * own, own), own)

    def block_copy(buf, l, d, sends, recvs, sender):
        region = buf.at[l, pl.ds(pl.multiple_of(sender * own, own), own)]
        return pltpu.make_async_remote_copy(
            src_ref=region, dst_ref=region,
            send_sem=sends.at[l, d - 1], recv_sem=recvs.at[l, d - 1],
            device_id={"dp": peer(d)}, device_id_type=MESH,
        )

    neighbours = not_first.astype(jnp.int32) + not_last.astype(jnp.int32) + (shards - 1)
    for l in range(layers):
        loads[l].wait()
        wfull[l, own_rows, :] = wst[l].astype(bf16)
        if l == 0:
            pl.semaphore_wait(barrier, neighbours)
        for d in range(1, shards):
            block_copy(wfull, l, d, w_send, w_recv, me).start()
    def columns(j, n=tile):
        return pl.ds(pl.multiple_of(j * n, n), n)

    def tile_copy(l, d, j, sender):
        region = vfull.at[l, pl.ds(pl.multiple_of(sender * own, own), own), columns(j, strip)]
        return pltpu.make_async_remote_copy(
            src_ref=region, dst_ref=region,
            send_sem=c_send.at[l - early, d - 1, j], recv_sem=c_recv.at[l - early, d - 1, j],
            device_id={"dp": peer(d)}, device_id_type=MESH,
        )

    loads[layers + 1].wait()
    for l in range(layers):
        vfull[l, own_rows, :] = (wst[l] - learn_rate * momentum_decay * mst[l]).astype(bf16)
    for l in range(early):
        for d in range(1, shards):
            block_copy(vfull, l, d, v_send, v_recv, me).start()
    for c in loads[layers:layers + 1] + loads[layers + 2:]:
        c.wait()

    def part(h):
        return pl.ds(pl.multiple_of(h * half, half), half)

    def landing(s):
        return me if s == SWEEPS - 1 else shards

    def hop(t, way, s, h, j):
        into = (xb, ab)[way]
        return pltpu.make_async_remote_copy(
            src_ref=stage.at[way, s, part(h), columns(j)],
            dst_ref=into.at[t, landing(s), part(h), columns(j)],
            send_sem=hop_send.at[t, way, s, h, j], recv_sem=hop_recv.at[t, way, s, h, j],
            device_id={"layer": g + 1 if way == 0 else g - 1}, device_id_type=MESH,
        )

    def strip_hop(t, j):
        return pltpu.make_async_remote_copy(
            src_ref=stage.at[0, 0, :, columns(j, strip)],
            dst_ref=xb.at[t, landing(0), :, columns(j, strip)],
            send_sem=strip_send.at[t, j], recv_sem=strip_recv.at[t, j],
            device_id={"layer": g + 1}, device_id_type=MESH,
        )

    def exchange_x(t, d, sender, h):
        region = xb.at[t, sender, part(h)]
        return pltpu.make_async_remote_copy(
            src_ref=region, dst_ref=region,
            send_sem=x_send.at[t, d - 1, h], recv_sem=x_recv.at[t, d - 1, h],
            device_id={"dp": peer(d)}, device_id_type=MESH,
        )

    def exchange_a(t, d, sender, h, j):
        region = ab.at[t, sender, part(h), columns(j)]
        return pltpu.make_async_remote_copy(
            src_ref=region, dst_ref=region,
            send_sem=a_send.at[t, d - 1, h, j], recv_sem=a_recv.at[t, d - 1, h, j],
            device_id={"dp": peer(d)}, device_id_type=MESH,
        )

    def take_x(t, s, h):
        if t == 0 or s > 0:
            @pl.when(not_first)
            def _():
                for j in range(tiles):
                    hop(t, 0, s, h, j).wait_recv()

        if s == SWEEPS - 1:
            for d in range(1, shards):
                exchange_x(t, d, me, h).start()

        @pl.when(not_first)
        def _():
            xcur[part(h), :] = xb[t, landing(s), part(h)].astype(f32)

    def take_a(t, s, h):
        for j in range(tiles):
            @pl.when(not_last)
            def _():
                hop(t, 1, s, h, j).wait_recv()

            if s == SWEEPS - 1:
                for d in range(1, shards):
                    exchange_a(t, d, me, h, j).start()

        @pl.when(not_last)
        def _():
            acur[part(h), :] = ab[t, landing(s), part(h)].astype(f32)

        @pl.when(is_last)
        def _():
            acur[part(h), :] = ab[t, me, part(h)].astype(f32)

    def fill(l, j):
        cols = columns(j, strip)

        @pl.loop(1, shards)
        def _(d):
            tile_copy(l, d, j, source(d)).wait_recv()
            there = pl.ds(pl.multiple_of(source(d) * own, own), own)
            fresh = vfull[l, there, cols].astype(f32) - pulls[l - early, there, cols]
            wfull[l, there, cols] = fresh.astype(bf16)

    def turn(l, j):
        @pl.loop(1, shards)
        def _(d):
            there = pl.ds(pl.multiple_of(source(d) * own, own), own)
            wturn[l, columns(j, strip), there] = wfull[l, there, columns(j, strip)].T

    everything = pl.ds(0, rows)

    def forward(here, first_in, first_x, keep, emit, filling=False):
        for l in range(layers):
            last = l == layers - 1
            source_ref = first_in if l == 0 else keep.at[l - 1]
            fills = filling and l >= early
            size = strip if fills else tile if last and emit is not None else width

            for j in range(width // size):
                if fills:
                    fill(l, j)

                cols = columns(j, size)
                product = jnp.dot(source_ref[here, :], wfull[l, :, cols], preferred_element_type=f32)
                squashed = jnp.tanh(product * width_scale)
                slopes[l, here, cols] = squashed
                before = first_x(here, cols) if l == 0 else xw[here, cols]
                after = before + step_size * squashed
                if last:
                    if emit is not None:
                        emit(j, cols, after)
                else:
                    xw[here, cols] = after
                    keep[l, here, cols] = after.astype(bf16)

                if fills:
                    turn(l, j)

    def backward(t, here, first_a, keep, emit):
        for l in reversed(range(layers)):
            start = first_a if l == layers - 1 else (lambda here, cols: xw[here, cols])

            every = pl.ds(0, width)
            slope = slopes[l, here, :]
            keep[l, here, :] = (start(here, every) * (1.0 - slope * slope)).astype(bf16)

            if l == 0 and emit is None:
                continue

            size = tile if l == 0 else width

            for j in range(width // size):
                cols = columns(j, size)
                if t > 0:
                    pulled = jnp.dot(
                        keep[l, here, :], wturn[l, :, cols], preferred_element_type=f32
                    )
                else:
                    pulled = lax.dot_general(
                        keep[l, here, :], wfull[l, cols, :], (((1,), (1,)), ((), ())),
                        preferred_element_type=f32,
                    )
                after = start(here, cols) + (step_size * width_scale) * pulled
                if l == 0:
                    emit(j, cols, after)
                else:
                    xw[here, cols] = after

    def own_x(here, cols):
        return xcur[here, cols]

    def own_a(here, cols):
        return acur[here, cols]

    for t in range(STEPS):
        own_mids = mids.at[me]
        own_sigs = sigs.at[me]
        if t == 0:
            for l in range(layers):
                for d in range(1, shards):
                    block_copy(wfull, l, d, w_send, w_recv, source(d)).wait_recv()

        @pl.when(is_first)
        def _():
            xb[t, me] = xcur[...].astype(bf16)

        def to_next(s, h, j):
            @pl.when(not_last)
            def _():
                hop(t, 0, s, h, j).start()

        if t > 0:
            in0[...] = xcur[...].astype(bf16)

            def emit(j, cols, after):
                stage[0, 0, :, cols] = after.astype(bf16)

                @pl.when(not_last)
                def _():
                    strip_hop(t, j).start()

            forward(everything, in0, own_x, own_mids, emit, True)

            @pl.when(not_first)
            def _():
                for j in range(strips):
                    strip_hop(t, j).wait_recv()

        for s in range(0 if t == 0 else 1, SWEEPS):
            @pl.loop(0, halves)
            def _(h):
                if s > 0:
                    take_x(t, s - 1, h)
                in0[part(h), :] = xcur[part(h), :].astype(bf16)

                def emit(j, cols, after):
                    stage[0, s, part(h), cols] = after.astype(bf16)
                    to_next(s, h, j)

                forward(part(h), in0, own_x, own_mids, emit)

        def pull_back(s, h):
            def emit(j, cols, after):
                stage[1, s, part(h), cols] = after.astype(bf16)

                @pl.when(not_first)
                def _():
                    hop(t, 1, s, h, j).start()

            backward(t, part(h), own_a, own_sigs, emit)

        @pl.loop(0, halves)
        def _(h):
            take_x(t, SWEEPS - 1, h)
            in0[part(h), :] = xcur[part(h), :].astype(bf16)
            if t == STEPS - 1:
                xs[me, part(h)] = in0[part(h), own_rows]

            def finals(j, cols, after):
                @pl.when(is_last)
                def _():
                    ab[t, me, part(h), cols] = (after - tgt[part(h), cols]).astype(bf16)

            forward(part(h), in0, own_x, own_mids, finals)
            pull_back(0, h)

        for s in range(1, SWEEPS):
            @pl.loop(0, halves)
            def _(h):
                take_a(t, s - 1, h)
                pull_back(s, h)

        @pl.loop(0, halves)
        def _(h):
            take_a(t, SWEEPS - 1, h)

        if t == 0:
            for l in range(early, layers):
                for j in range(strips):
                    for d in range(1, shards):
                        tile_copy(l, d, j, me).start()
        backward(t, everything, own_a, own_sigs, None)

        if t == STEPS - 1:
            for l in range(layers):
                left = xs[me] if l == 0 else mids[me, l - 1, :, own_rows]
                mst[l] = momentum_decay * mst[l] + row_scale * lax.dot_general(
                    left, sigs[me, l], (((0,), (0,)), ((), ())), preferred_element_type=f32
                )

        @pl.loop(1, shards)
        def _(d):
            s = source(d)
            for h in range(halves):
                exchange_x(t, d, s, h).wait_recv()
            if t == STEPS - 1:
                xs[s] = xb[t, s, :, own_rows]
            forward(
                everything, xb.at[t, s], lambda here, cols: xb[t, s, here, cols].astype(f32),
                mids.at[s], None,
            )

            @pl.loop(0, halves)
            def _(h):
                for j in range(tiles):
                    exchange_a(t, d, s, h, j).wait_recv()
                backward(
                    t, part(h), lambda here, cols: ab[t, s, here, cols].astype(f32), sigs.at[s], None
                )

        if t == 0:
            for l in range(layers):
                for d in range(1, shards):
                    block_copy(wfull, l, d, w_send, w_recv, me).wait_send()

        def gradient(l, at):
            feats = pl.ds(pl.multiple_of(at, own), own)
            if l == 0:
                left = xb[t, 0:shards, :, feats].reshape(shards * rows, own)
            else:
                left = mids[:, l - 1, :, feats].reshape(shards * rows, own)
            right = sigs[:, l].reshape(shards * rows, width)
            return lax.dot_general(
                left, right, (((0,), (0,)), ((), ())), preferred_element_type=f32
            ) * row_scale

        for l in range(layers if t < STEPS - 1 else 0):
            moved = momentum_decay * mst[l] + gradient(l, me * own)
            mst[l] = moved
            fresh = wst[l] - learn_rate * moved
            wst[l] = fresh
            wfull[l, own_rows, :] = fresh.astype(bf16)
            wturn[l, :, own_rows] = wfull[l, own_rows, :].T

        for l in range(layers if t < STEPS - 1 else 0):
            @pl.loop(1, shards)
            def _(d):
                there = pl.ds(pl.multiple_of(source(d) * own, own), own)
                pull = learn_rate * gradient(l, source(d) * own)
                if l < early:
                    block_copy(vfull, l, d, v_send, v_recv, source(d)).wait_recv()
                    wfull[l, there, :] = (vfull[l, there, :].astype(f32) - pull).astype(bf16)
                    wturn[l, :, there] = wfull[l, there, :].T
                else:
                    pulls[l - early, there, :] = pull

        @pl.loop(0, halves)
        def _(h):
            for s in range(SWEEPS):
                for j in range(tiles):
                    if t == 0 or s > 0:
                        @pl.when(not_last)
                        def _():
                            hop(t, 0, s, h, j).wait_send()

                    @pl.when(not_first)
                    def _():
                        hop(t, 1, s, h, j).wait_send()

            for d in range(1, shards):
                exchange_x(t, d, me, h).wait_send()
                for j in range(tiles):
                    exchange_a(t, d, me, h, j).wait_send()

        if t > 0:
            @pl.when(not_last)
            def _():
                for j in range(strips):
                    strip_hop(t, j).wait_send()

    for d in range(1, shards):
        for l in range(early):
            block_copy(vfull, l, d, v_send, v_recv, me).wait_send()
        for l in range(early, layers):
            for j in range(strips):
                tile_copy(l, d, j, me).wait_send()


def finish(w, m, x, a, xs, mids, sigs, w_out, m_out, b_out, a_out, w_new, m_new, sem):
    layers, own, width = w.shape
    shards, rows, _ = mids.shape[0], *mids.shape[2:]
    part = min(128, own)
    me = lax.axis_index("dp")
    row_scale = 1.0 / math.sqrt(rows * shards)
    copies = [
        pltpu.make_async_copy(x, b_out.at[0], sem.at[0]),
        pltpu.make_async_copy(a, a_out.at[0], sem.at[1]),
    ]
    for c in copies:
        c.start()
    for l in range(layers):
        for i in range(own // part):
            here = pl.ds(i * part, part)
            feats = pl.ds(pl.multiple_of(me * own + i * part, part), part)
            moved = m[l, here, :]
            for d in range(1, shards):
                other = lax.rem(me + shards - d, shards)
                left = xs[other, :, here] if l == 0 else mids[other, l - 1, :, feats]
                moved += row_scale * lax.dot_general(
                    left, sigs[other, l], (((0,), (0,)), ((), ())), preferred_element_type=f32
                )
            m_new[l, here, :] = moved
            w_new[l, here, :] = w[l, here, :] - learn_rate * moved
            at = 2 + 2 * (l * (own // part) + i)
            for k, (new, out) in enumerate(((m_new, m_out), (w_new, w_out))):
                c = pltpu.make_async_copy(new.at[l, here], out.at[l, here], sem.at[at + k])
                c.start()
                copies.append(c)
    for c in copies:
        c.wait()


def size_of(refs):
    return sum(math.prod(r.shape) * jnp.dtype(r.dtype).itemsize for r in refs)


def local(groups, shards, weights, momentum, boundary, adjoint, target):
    layers, own, width = weights.shape
    rows = target.shape[0]
    tiles = width // min(512, width)
    strips = width // min(256, width)
    halves = 2 if rows % 64 == 0 else 1
    early = layers // 2
    others = max(shards - 1, 1)
    dma = pltpu.SemaphoreType.DMA
    anywhere = pl.BlockSpec(memory_space=pl.ANY)
    inside = pl.BlockSpec(memory_space=pltpu.VMEM)
    kept = (
        pltpu.VMEM((layers, own, width), f32),
        pltpu.VMEM((layers, own, width), f32),
        pltpu.VMEM((rows, width), f32),
        pltpu.VMEM((rows, width), f32),
        pltpu.VMEM((shards, rows, own), bf16),
        pltpu.VMEM((shards, max(layers - 1, 1), rows, width), bf16),
        pltpu.VMEM((shards, layers, rows, width), bf16),
    )
    scratch = [
        pltpu.VMEM((layers, width, width), bf16),
        pltpu.VMEM((layers, width, width), bf16),
        pltpu.VMEM((layers, width, width), bf16),
        pltpu.VMEM((layers - early, width, width), f32),
        pltpu.VMEM((rows, width), f32),
        pltpu.VMEM((rows, width), f32),
        pltpu.VMEM((rows, width), bf16),
        pltpu.VMEM((layers, rows, width), f32),
        pltpu.VMEM((STEPS, shards + 1, rows, width), bf16),
        pltpu.VMEM((STEPS, shards + 1, rows, width), bf16),
        pltpu.VMEM((2, SWEEPS, rows, width), bf16),
    ]
    state = pl.pallas_call(
        functools.partial(kernel, groups, shards),
        out_shape=kept,
        in_specs=[pl.BlockSpec(memory_space=pltpu.HBM)] * 5,
        out_specs=(inside,) * len(kept),
        scratch_shapes=scratch + [
            dma((layers + 4,)),
            dma((layers, others)),
            dma((layers, others)),
            dma((layers, others)),
            dma((layers, others)),
            dma((layers - early, others, strips)),
            dma((layers - early, others, strips)),
            dma((STEPS, 2, SWEEPS, halves, tiles)),
            dma((STEPS, 2, SWEEPS, halves, tiles)),
            dma((STEPS, strips)),
            dma((STEPS, strips)),
            dma((STEPS, others, halves)),
            dma((STEPS, others, halves)),
            dma((STEPS, others, halves, tiles)),
            dma((STEPS, others, halves, tiles)),
        ],
        name="relax",
        compiler_params=pltpu.CompilerParams(
            collective_id=0, has_side_effects=True,
            vmem_limit_bytes=min(size_of(scratch) + 12 * 2**20, 63 * 2**20 - size_of(kept)),
        ),
    )(*(pltpu.with_memory_space_constraint(v, pltpu.HBM) for v in (weights, momentum, boundary, adjoint, target)))
    fresh = [pltpu.VMEM((layers, own, width), f32)] * 2
    return pl.pallas_call(
        finish,
        out_shape=tuple(
            jax.ShapeDtypeStruct(v.shape, f32) for v in (weights, momentum, boundary, adjoint)
        ),
        in_specs=[inside] * len(kept),
        out_specs=(anywhere,) * 4,
        scratch_shapes=fresh + [dma((2 + 2 * layers * max(own // 128, 1),))],
        name="finish",
        compiler_params=pltpu.CompilerParams(
            vmem_limit_bytes=size_of(fresh) + 8 * 1024 * 1024,
        ),
    )(*state)


def solution(mesh):
    placed = P("layer", "dp", None)
    return jax.shard_map(
        functools.partial(local, mesh.shape["layer"], mesh.shape["dp"]),
        mesh=mesh,
        in_specs=(placed,) * 4 + (P("dp", None),),
        out_specs=(placed,) * 4,
        check_vma=False,
    )
```
